32 devices in a mesh: chan: 4 (over y, core), lon: 8 (over z, x).
Axes of the slice: x: 2, y: 2, z: 4, core: 2. Of those that a mesh axis runs over, the one named last changes fastest.
Arguments:
- patches: bfloat16 [32, 32, 64, 128], P('chan', None, 'lon'), may hold values from -6 to 6
- embed_weight: bfloat16 [32, 128, 256], P('chan'), may hold values from -0.5 to 0.5
- channel_embed: bfloat16 [32, 256], P('chan'), may hold values from -6 to 6
- agg_query: float32 [256], replicated, may hold values from -160 to 160
- norm_gains: float32 [5, 256], replicated, may hold values from 0.25 to 1.75
- qkv_weight: bfloat16 [2, 256, 768], P(None, None, 'lon'), may hold values from -0.375 to 0.375
- proj_weight: bfloat16 [2, 256, 256], P(None, 'lon'), may hold values from -0.375 to 0.375
- up_weight: bfloat16 [2, 256, 1024], P(None, None, 'lon'), may hold values from -0.375 to 0.375
- down_weight: bfloat16 [2, 1024, 256], P(None, 'lon'), may hold values from -0.1875 to 0.1875
- decode_weight: bfloat16 [32, 256, 128], P('chan'), may hold values from -0.375 to 0.375
Outputs:
- decoded: bfloat16 [32, 32, 64, 128], P('chan', None, 'lon')
The draws below stay inside these ranges and needn't reach their ends.
All inputs are finite; a program needn't handle non-finite values.
Results may differ from the reference program's by a relative error of at most 0.018.
Values may be sent and summed in bfloat16 or wider, within the bound.
A program may use at most 64 MiB of HBM per device.

```python
import jax
import jax.numpy as jnp
from jax import lax

C = 32
P_SIZE = 128
E = 256
H = 1024
HEADS = 8
WR = 8
WC = 8
ROWS = 32
LONS = 64


def draw_agg_query(key, part):
    base = jnp.clip(jax.random.normal(key, (E,), jnp.float32), -4.0, 4.0)
    return base


def block_levels(rng, shape, cuts, least, top_value):
    loudness, own = 1.0, jax.random.fold_in(rng, 6)
    for axis_at, shards_of in cuts:
        draws = jnp.exp(jax.random.uniform(jax.random.fold_in(own, axis_at), (shards_of,), jnp.float32, least / len(cuts), top_value / len(cuts)))
        loudness = loudness * jnp.repeat(draws, shape[axis_at] // shards_of).reshape([-1 if axis == axis_at else 1 for axis in range(len(shape))])
    return loudness


def bell_draw(key, dims, deviation, bound, split=(), kind=jnp.bfloat16):
    level = block_levels(key, dims, split, -0.22, 0.18) if split else 1.0
    array = jax.random.normal(key, dims, jnp.float32) * deviation * level
    return jnp.minimum(jnp.maximum(array, -bound), bound).astype(kind)


def setup_inputs(seed: int = 0) -> dict:
    key_of = jax.random.split(jax.random.key(seed), 11)
    patches = bell_draw(key_of[0], (C, ROWS, LONS, P_SIZE), 1.0, 6.0, ((0, 4), (2, 8)))
    embed_weight = bell_draw(key_of[1], (C, P_SIZE, E), P_SIZE ** -0.5, 0.5, ((0, 4),))
    channel_embed = bell_draw(key_of[2], (C, E), 1.0, 6.0, ((0, 4),))
    agg_query = draw_agg_query(jax.random.fold_in(key_of[10], 71), 0)
    norm_gains = jnp.clip(1.0 + 0.15 * jax.random.normal(key_of[4], (5, E), jnp.float32), 0.25, 1.75)
    qkv_weight = bell_draw(key_of[5], (2, E, 3 * E), E ** -0.5, 0.375, ((2, 8),))
    proj_weight = bell_draw(key_of[6], (2, E, E), E ** -0.5, 0.375, ((1, 8),))
    up_weight = bell_draw(key_of[7], (2, E, H), E ** -0.5, 0.375, ((2, 8),))
    down_weight = bell_draw(key_of[8], (2, H, E), H ** -0.5, 0.1875, ((1, 8),))
    decode_weight = bell_draw(key_of[9], (C, E, P_SIZE), E ** -0.5, 0.375, ((0, 4),))
    return {"patches": patches, "embed_weight": embed_weight, "channel_embed": channel_embed, "agg_query": agg_query, "norm_gains": norm_gains, "qkv_weight": qkv_weight, "proj_weight": proj_weight, "up_weight": up_weight, "down_weight": down_weight, "decode_weight": decode_weight}


EPS = 1e-05

def layer_norm(values, gain):
    mean = lax.optimization_barrier(jnp.mean(values, axis=-1, keepdims=True))
    centred = values - mean
    spread = lax.optimization_barrier(jnp.mean(centred * centred, axis=-1, keepdims=True))
    return centred * lax.rsqrt(spread + EPS) * gain

def window_block(windows, gain_attn, gain_mlp, w_qkv, w_proj, w_up, w_down):
    count, length, width = windows.shape
    head_dim = width // HEADS
    flat = windows.reshape(count * length, width)
    normed = layer_norm(flat, gain_attn).astype(jnp.bfloat16)
    qkv = jnp.dot(normed, w_qkv, preferred_element_type=jnp.float32).astype(jnp.bfloat16)
    qkv = lax.optimization_barrier(qkv)
    qkv = qkv.reshape(count, length, 3, HEADS, head_dim).astype(jnp.float32)
    scores = jnp.einsum('nqhd,nkhd->nhqk', qkv[:, :, 0], qkv[:, :, 1]) * head_dim ** (-0.5)
    probs = jax.nn.softmax(scores, axis=-1).astype(jnp.bfloat16)
    probs = lax.optimization_barrier(probs).astype(jnp.float32)
    mixed = jnp.einsum('nhqk,nkhd->nqhd', probs, qkv[:, :, 2]).astype(jnp.bfloat16)
    mixed = mixed.reshape(count * length, width)
    state = flat + jnp.dot(mixed, w_proj, preferred_element_type=jnp.float32)
    normed = layer_norm(state, gain_mlp).astype(jnp.bfloat16)
    hidden = jax.nn.gelu(jnp.dot(normed, w_up, preferred_element_type=jnp.float32)).astype(jnp.bfloat16)
    state = state + jnp.dot(hidden, w_down, preferred_element_type=jnp.float32)
    return state.reshape(count, length, width)

def apply_block(grid, layer, offset, norm_gains, qkv_weight, proj_weight, up_weight, down_weight):
    rows, cols, width = grid.shape
    rolled = jnp.roll(grid, -offset, axis=1)
    windows = rolled.reshape(rows // WR, WR, cols // WC, WC, width).transpose(0, 2, 1, 3, 4)
    windows = windows.reshape(-1, WR * WC, width)
    result = window_block(windows, norm_gains[2 * layer], norm_gains[2 * layer + 1], qkv_weight[layer], proj_weight[layer], up_weight[layer], down_weight[layer])
    result = result.reshape(rows // WR, cols // WC, WR, WC, width).transpose(0, 2, 1, 3, 4)
    return jnp.roll(result.reshape(rows, cols, width), offset, axis=1)

def reference(patches, embed_weight, channel_embed, agg_query, norm_gains, qkv_weight, proj_weight, up_weight, down_weight, decode_weight):
    count = ROWS * LONS
    flat = patches.reshape(C, count, P_SIZE)
    query_proj = jnp.einsum('cpe,e->cp', embed_weight.astype(jnp.float32), agg_query, precision=lax.Precision.HIGHEST)
    bias_score = jnp.dot(channel_embed.astype(jnp.float32), agg_query, precision=lax.Precision.HIGHEST)

    def channel_score(index):
        piece = flat[index].astype(jnp.float32)
        return jnp.dot(piece, query_proj[index], precision=lax.Precision.HIGHEST) + bias_score[index]
    scores = lax.map(channel_score, jnp.arange(C, dtype=jnp.int32)) * E ** (-0.5)
    top = lax.optimization_barrier(jnp.max(scores, axis=0))
    shares = jnp.exp(scores - top[None])
    denom = lax.optimization_barrier(jnp.sum(shares, axis=0))

    def accumulate(total, index):
        embedded = jnp.dot(flat[index], embed_weight[index], preferred_element_type=jnp.float32)
        embedded = embedded + channel_embed[index].astype(jnp.float32)[None]
        return (total + shares[index][:, None] * embedded, None)
    numer, _ = lax.scan(accumulate, jnp.zeros((count, E), jnp.float32), jnp.arange(C, dtype=jnp.int32))
    grid = (numer / denom[:, None]).reshape(ROWS, LONS, E)
    grid = apply_block(grid, 0, 0, norm_gains, qkv_weight, proj_weight, up_weight, down_weight)
    grid = apply_block(grid, 1, WC // 2, norm_gains, qkv_weight, proj_weight, up_weight, down_weight)
    final = layer_norm(grid.reshape(count, E), norm_gains[4]).astype(jnp.bfloat16)

    def decode(index):
        return jnp.dot(final, decode_weight[index], preferred_element_type=jnp.float32).astype(jnp.bfloat16)
    decoded = lax.map(decode, jnp.arange(C, dtype=jnp.int32))
    return decoded.reshape(C, ROWS, LONS, P_SIZE)
```

```python
import functools

import jax
import jax.numpy as jnp
from jax import lax
from jax.experimental import pallas as pl
from jax.experimental.pallas import tpu as pltpu
from jax.sharding import PartitionSpec as P

HEADS = 8
WC = 8
EPS = 1e-05
MESH = pl.DeviceIdType.MESH
BF16 = jnp.bfloat16
F32 = jnp.float32
NT = (((1,), (1,)), ((), ()))


def layer_norm(values, gain):
    mean = jnp.mean(values, axis=-1, keepdims=True)
    centred = values - mean
    spread = jnp.mean(centred * centred, axis=-1, keepdims=True)
    return centred * lax.rsqrt(spread + EPS) * gain


def merged(block):
    shards, rows, width = block.shape
    if rows % 16:
        return block.astype(F32).reshape(shards * rows, width).astype(BF16)
    return block.reshape(shards * rows, width)


def inner_factor(count):
    inner = 1
    while inner * inner * 4 <= count:
        inner *= 2
    return inner if count % inner == 0 else 1


class Sems:
    def __init__(self, ref=None):
        self.ref, self.used = ref, 0

    def take(self):
        self.used += 1
        return None if self.ref is None else self.ref.at[self.used - 1]


class Gather:
    def __init__(self, buf, geometry, x_first, sends, recvs):
        self.buf = buf
        self.geometry, self.x_first = geometry, x_first
        self.sends, self.recvs = sends, recvs
        self.pending = []
        self.late = []

    def rows(self, core):
        half = self.buf.shape[1] // 2
        return pl.ds(pl.multiple_of(core * half, half), half)

    def copy(self, first, count, core, target, sem_pair):
        piece = self.buf.at[pl.ds(first, count), self.rows(core)]
        return pltpu.make_async_remote_copy(
            src_ref=piece,
            dst_ref=piece,
            send_sem=sem_pair[0],
            recv_sem=sem_pair[1],
            device_id=target,
            device_id_type=MESH,
        )

    def pair(self):
        return self.sends.take(), self.recvs.take()

    def begin(self, copy, when=None):
        if when is None:
            copy.start()
        else:
            pl.when(when)(copy.start)
        self.pending.append((copy, when))

    def arrive(self, copy, when=None):
        if when is None:
            copy.wait_recv()
        else:
            pl.when(when)(copy.wait_recv)

    def share(self, first, count, when=None):
        g = self.geometry
        pair = self.pair()
        self.begin(self.copy(first, count, g["core"], g["partner"], pair), when)
        self.late.append((self.copy(first, count, 1 - g["core"], g["partner"], pair), when))

    def across(self, z, when=None):
        g = self.geometry
        inner, x, core = g["inner"], g["x"], g["core"]
        incoming = []
        for step in range(1, inner):
            pair = self.pair()
            to, source = lax.rem(x + step, inner), lax.rem(x + inner - step, inner)
            peer = g["at"](g["z"], to)
            self.begin(self.copy(z * inner + x, 1, core, peer, pair), when)
            incoming.append((z * inner + source, self.copy(z * inner + source, 1, core, peer, pair), when))
        return incoming

    def steps(self):
        g = self.geometry
        inner, outer, x, z, core = g["inner"], g["outer"], g["x"], g["z"], g["core"]
        width = inner if self.x_first else 1

        def first_of(at):
            return at * inner if self.x_first else at * inner + x

        if self.x_first:
            incoming = self.across(z)
            yield
            for _, copy, when in incoming:
                self.arrive(copy, when)
            for shard, _, when in incoming:
                self.share(shard, 1, when)
        crossing = []
        for step in range(outer):
            if step < outer - 1:
                right, left = self.pair(), self.pair()
                here_right = (z + 1 < outer) & (z - step >= 0)
                here_left = (z - 1 >= 0) & (z + step < outer)
                at_right, at_left = jnp.maximum(z - step, 0), jnp.minimum(z + step, outer - 1)
                up, down = jnp.minimum(z + 1, outer - 1), jnp.maximum(z - 1, 0)
                self.begin(self.copy(first_of(at_right), width, core, g["at"](up, x), right), here_right)
                self.begin(self.copy(first_of(at_left), width, core, g["at"](down, x), left), here_left)
            if step == 0:
                arrived = [(z, None)]
            for at, when in arrived:
                if not self.x_first:
                    crossing += self.across(at, when)
                if step:
                    self.share(first_of(at), width, when)
            if step == outer - 1:
                break
            yield
            from_left, from_right = z - 1 - step >= 0, z + 1 + step < outer
            at_left, at_right = jnp.maximum(z - 1 - step, 0), jnp.minimum(z + 1 + step, outer - 1)
            self.arrive(self.copy(first_of(at_left), width, core, g["at"](down, x), right), from_left)
            self.arrive(self.copy(first_of(at_right), width, core, g["at"](up, x), left), from_right)
            arrived = [(at_left, from_left), (at_right, from_right)]
        for shard, copy, when in crossing:
            yield
            self.arrive(copy, when)
            self.share(shard, 1, when)
        yield
        for copy, when in self.late:
            self.arrive(copy, when)

    def finish(self):
        for copy, when in self.pending:
            if when is None:
                copy.wait_send()
            else:
                pl.when(when)(copy.wait_send)


def window_block(state, gain_attn, gain_mlp, attn_ref, mlp_ref, sizes):
    n_qkv, n_up = sizes
    length, width = state.shape
    head_dim = width // HEADS
    normed = layer_norm(state, gain_attn).astype(BF16)
    w_qkv = merged(attn_ref[:, :n_qkv])
    qkv = lax.dot_general(normed, w_qkv, NT, preferred_element_type=F32).astype(BF16)
    query, key, value = (qkv[:, i * width : (i + 1) * width] for i in range(3))
    head = lax.broadcasted_iota(jnp.int32, (length, width), 1) // head_dim
    zero = jnp.zeros((), F32)
    wide = query.astype(F32)
    stacked = jnp.concatenate(
        [jnp.where(head == h, wide, zero).astype(BF16) for h in range(HEADS)], axis=0
    )
    scores = lax.dot_general(stacked, key, NT, preferred_element_type=F32) * head_dim ** (-0.5)
    scores = jnp.exp(scores - jnp.max(scores, axis=-1, keepdims=True))
    probs = (scores / jnp.sum(scores, axis=-1, keepdims=True)).astype(BF16)
    every = jnp.dot(probs, value, preferred_element_type=F32)
    mixed = jnp.zeros((length, width), F32)
    for h in range(HEADS):
        mixed = jnp.where(head == h, every[h * length : (h + 1) * length], mixed)
    w_proj = merged(attn_ref[:, n_qkv:])
    state = state + jnp.dot(mixed.astype(BF16), w_proj, preferred_element_type=F32)
    normed = layer_norm(state, gain_mlp).astype(BF16)
    w_up = merged(mlp_ref[:, :n_up])
    hidden = lax.dot_general(normed, w_up, NT, preferred_element_type=F32)
    hidden = jax.nn.gelu(hidden).astype(BF16)
    w_down = merged(mlp_ref[:, n_up:])
    return state + jnp.dot(hidden, w_down, preferred_element_type=F32)


def sem_count(outer, inner, x_first):
    moves = 2 * (outer - 1)
    if x_first:
        return 2 * (inner - 1) + 2 * moves
    return 2 * moves + (1 + moves) * (inner - 1) * 2


def kernel(
    groups, lons, inner, sizes,
    patches, embed_weight, channel_embed, agg_query, gains, packed, decode_weight,
    out,
    embedded, partial, aux_out, aux_in, mean_in, attn0, mlp0, attn1, mlp1, edge_out, edge_in, final_out, final_in,
    chunk_send, chunk_recv, own_sem, agg_send, agg_recv, aux_send, aux_recv, edge_send, edge_recv, fin_send, fin_recv,
):
    chans, count, _ = patches.shape
    width = embed_weight.shape[2]
    owned = count // groups
    half = owned // 2
    me, lon = lax.axis_index("chan"), lax.axis_index("lon")
    west, east = lax.rem(lon + lons - 1, lons), lax.rem(lon + 1, lons)
    barrier = pltpu.get_barrier_semaphore()
    greeted = 0
    for step in range(1, lons):
        pl.semaphore_signal(barrier, inc=1, device_id=(me, lax.rem(lon + step, lons)), device_id_type=MESH)
        greeted += 1
    for step in range(1, groups):
        other = lax.rem(me + step, groups)
        for column in (lon, west, east):
            pl.semaphore_signal(barrier, inc=1, device_id=(other, column), device_id_type=MESH)
            greeted += 1

    n_qkv, n_proj, n_up, n_down = sizes
    n_attn = n_qkv + n_proj
    core = lax.rem(me, 2)
    outer = lons // inner
    geometry = {
        "inner": inner, "outer": outer, "core": core,
        "x": lax.rem(lon, inner), "z": lon // inner,
        "partner": (me + 1 - 2 * core, lon),
        "at": lambda z, x: (me, z * inner + x),
    }
    bufs = (attn0, mlp0, attn1, mlp1)
    own_copies = []
    for at, buf in enumerate(bufs):
        layer, rows = at // 2, pl.ds(0, n_attn) if at % 2 == 0 else pl.ds(n_attn, n_up + n_down)
        copy = pltpu.make_async_copy(packed.at[layer, rows], buf.at[lon], own_sem.at[at])
        copy.start()
        own_copies.append(copy)

    query = agg_query[...]
    scores = []
    for c in range(chans):
        value = jnp.dot(patches[c], embed_weight[c], preferred_element_type=F32)
        value = value + channel_embed[c : c + 1].astype(F32)
        embedded[c] = value
        scores.append(jnp.sum(value * query, axis=-1, keepdims=True) * width ** (-0.5))

    for copy in own_copies:
        copy.wait()
    pl.semaphore_wait(barrier, greeted)

    offset, gathers = 0, []
    for at, order in enumerate((True, False, False, True)):
        pairs = sem_count(outer, inner, order)
        sends, recvs = Sems(chunk_send.at[pl.ds(offset, pairs)]), Sems(chunk_recv.at[pl.ds(offset, pairs)])
        gathers.append(Gather(bufs[at], geometry, order, sends, recvs))
        offset += pairs
    flows = [one.steps() for one in gathers]
    for flow in flows:
        next(flow)

    top = functools.reduce(jnp.maximum, scores)
    shares = [jnp.exp(score - top) for score in scores]
    denom = functools.reduce(jnp.add, shares)
    lane = lax.broadcasted_iota(jnp.int32, (count, 128), 1)
    aux = jnp.where(lane == 0, top, jnp.where(lane == 1, denom, 0.0))
    numer = shares[0] * embedded[0]
    for c in range(1, chans):
        numer = numer + shares[c] * embedded[c]
    mean = numer / denom
    for g in range(groups):
        partial[g] = mean[g * owned : (g + 1) * owned].astype(BF16)
        block = aux[g * owned : (g + 1) * owned]
        if owned < 128:
            block = jnp.concatenate([block, jnp.zeros((128 - owned, 128), F32)], axis=0)
        aux_out[g] = block.T[:8]
    sent = []
    for step in range(1, groups):
        to = lax.rem(me + step, groups)
        sent.append(
            pltpu.make_async_remote_copy(
                src_ref=partial.at[to], dst_ref=mean_in.at[step - 1],
                send_sem=agg_send.at[step - 1], recv_sem=agg_recv.at[step - 1],
                device_id=(to, lon), device_id_type=MESH,
            )
        )
        sent.append(
            pltpu.make_async_remote_copy(
                src_ref=aux_out.at[to], dst_ref=aux_in.at[step - 1],
                send_sem=aux_send.at[step - 1], recv_sem=aux_recv.at[step - 1],
                device_id=(to, lon), device_id_type=MESH,
            )
        )
    for copy in sent:
        copy.start()

    def drain(*which):
        live = [flows[i] for i in which]
        while live:
            for flow in list(live):
                if next(flow, "end") == "end":
                    live.remove(flow)

    drain(0, 1)

    for copy in sent:
        copy.wait_recv()
    means = [partial[me].astype(F32)] + [mean_in[i].astype(F32) for i in range(groups - 1)]
    columns = [aux_out[me].T] + [aux_in[i].T for i in range(groups - 1)]
    tops = [column[:owned, 0:1] for column in columns]
    best = functools.reduce(jnp.maximum, tops)
    weights = [column[:owned, 1:2] * jnp.exp(one - best) for column, one in zip(columns, tops)]
    total = functools.reduce(jnp.add, weights)
    state = functools.reduce(jnp.add, [w * m for w, m in zip(weights, means)]) / total

    side = WC // 2

    def order_matrix(flip, kind):
        row = lax.broadcasted_iota(jnp.int32, (owned, owned), 1 if flip else 0)
        token = lax.broadcasted_iota(jnp.int32, (owned, owned), 0 if flip else 1)
        within = row % half
        return jnp.where((within // side) * WC + (row // half) * side + within % side == token, 1.0, 0.0).astype(kind)

    state = jnp.dot(order_matrix(False, F32), state, precision=lax.Precision.HIGHEST, preferred_element_type=F32)

    def gain(i):
        return gains[i : i + 1]

    state = window_block(state, gain(0), gain(1), attn0, mlp0, (n_qkv, n_up))
    edge_out[...] = state[:half].astype(BF16)
    edge = pltpu.make_async_remote_copy(
        src_ref=edge_out, dst_ref=edge_in, send_sem=edge_send.at[0], recv_sem=edge_recv.at[0],
        device_id=(me, west), device_id_type=MESH,
    )
    edge.start()
    drain(2, 3)
    edge.wait_recv()
    moved = jnp.concatenate([state[half:], edge_in[...].astype(F32)], axis=0)
    moved = window_block(moved, gain(2), gain(3), attn1, mlp1, (n_qkv, n_up))
    final = layer_norm(moved, gain(4)).astype(BF16)
    final_out[0] = final[half:]
    final_out[1] = final[:half]
    last = []
    for step in range(groups):
        to = lax.rem(me + step, groups)
        last.append(
            pltpu.make_async_remote_copy(
                src_ref=final_out.at[0], dst_ref=final_in.at[me, 0],
                send_sem=fin_send.at[step, 0], recv_sem=fin_recv.at[step, 0],
                device_id=(to, east), device_id_type=MESH,
            )
        )
        if step:
            last.append(
                pltpu.make_async_remote_copy(
                    src_ref=final_out.at[1], dst_ref=final_in.at[me, 1],
                    send_sem=fin_send.at[step, 1], recv_sem=fin_recv.at[step, 1],
                    device_id=(to, lon), device_id_type=MESH,
                )
            )
    for copy in last:
        copy.start()
    final_in[me, 1] = final[:half]
    arrivals = []
    for step in range(groups):
        source = lax.rem(me + groups - step, groups)
        for part in range(2):
            if step or part == 0:
                pltpu.make_async_remote_copy(
                    src_ref=final_out.at[part], dst_ref=final_in.at[source, part],
                    send_sem=fin_send.at[step, part], recv_sem=fin_recv.at[step, part],
                    device_id=(source, west if part == 0 else lon) if step else (me, west), device_id_type=MESH,
                ).wait_recv()
    back = order_matrix(True, BF16)
    tokens = []
    for g in range(groups):
        both = merged(final_in[g])
        tokens.append(jnp.dot(back, both, preferred_element_type=F32).astype(BF16))
    tokens = jnp.concatenate(tokens, axis=0)
    for c in range(chans):
        out[c] = jnp.dot(tokens, decode_weight[c], preferred_element_type=F32).astype(BF16)

    for one in gathers:
        one.finish()
    for copy in sent + [edge] + last:
        copy.wait_send()


def body(
    patches, embed_weight, channel_embed, agg_query, norm_gains,
    qkv_weight, proj_weight, up_weight, down_weight, decode_weight,
):
    chans, rows, cols, width_p = patches.shape
    width = embed_weight.shape[2]
    count = rows * cols
    groups, lons = lax.axis_size("chan"), lax.axis_size("lon")
    owned = count // groups
    half = owned // 2
    assert cols == WC and owned <= 128
    packed = jnp.concatenate(
        [qkv_weight.transpose(0, 2, 1), proj_weight, up_weight.transpose(0, 2, 1), down_weight], axis=1
    )
    sizes = (qkv_weight.shape[2], proj_weight.shape[1], up_weight.shape[2], down_weight.shape[1])
    n_attn, n_mlp = sizes[0] + sizes[1], sizes[2] + sizes[3]
    inner = inner_factor(lons)
    outer = lons // inner
    pairs = sum(sem_count(outer, inner, order) for order in (True, False, False, True))
    vmem = pl.BlockSpec(memory_space=pltpu.VMEM)
    out = pl.pallas_call(
        functools.partial(kernel, groups, lons, inner, sizes),
        out_shape=jax.ShapeDtypeStruct((chans, count, decode_weight.shape[2]), BF16),
        in_specs=[vmem] * 7,
        out_specs=vmem,
        scratch_shapes=[
            pltpu.VMEM((chans, count, width), F32),
            pltpu.VMEM((groups, owned, width), BF16),
            pltpu.VMEM((groups, 8, 128), F32),
            pltpu.VMEM((groups - 1, 8, 128), F32),
            pltpu.VMEM((groups - 1, owned, width), BF16),
            pltpu.VMEM((lons, n_attn, width), BF16),
            pltpu.VMEM((lons, n_mlp, width), BF16),
            pltpu.VMEM((lons, n_attn, width), BF16),
            pltpu.VMEM((lons, n_mlp, width), BF16),
            pltpu.VMEM((half, width), BF16),
            pltpu.VMEM((half, width), BF16),
            pltpu.VMEM((2, half, width), BF16),
            pltpu.VMEM((groups, 2, half, width), BF16),
            pltpu.SemaphoreType.DMA((pairs,)),
            pltpu.SemaphoreType.DMA((pairs,)),
            pltpu.SemaphoreType.DMA((4,)),
            pltpu.SemaphoreType.DMA((groups - 1,)),
            pltpu.SemaphoreType.DMA((groups - 1,)),
            pltpu.SemaphoreType.DMA((groups - 1,)),
            pltpu.SemaphoreType.DMA((groups - 1,)),
            pltpu.SemaphoreType.DMA((1,)),
            pltpu.SemaphoreType.DMA((1,)),
            pltpu.SemaphoreType.DMA((groups, 2)),
            pltpu.SemaphoreType.DMA((groups, 2)),
        ],
        compiler_params=pltpu.CompilerParams(
            collective_id=0, has_side_effects=True, vmem_limit_bytes=60 * 1024 * 1024
        ),
    )(
        patches.reshape(chans, count, width_p), embed_weight, channel_embed, agg_query.reshape(1, width),
        norm_gains, packed, decode_weight,
    )
    return out.reshape(chans, rows, cols, -1)


def solution(mesh):
    placed = (
        P("chan", None, "lon", None),
        P("chan", None, None),
        P("chan", None),
        P(),
        P(),
        P(None, None, "lon"),
        P(None, "lon", None),
        P(None, None, "lon"),
        P(None, "lon", None),
        P("chan", None, None),
    )
    return jax.shard_map(
        body, mesh=mesh, in_specs=placed, out_specs=P("chan", None, "lon", None), check_vma=False
    )
```

```python
import functools

import jax
import jax.numpy as jnp
from jax import lax
from jax.experimental import pallas as pl
from jax.experimental.pallas import tpu as pltpu
from jax.sharding import PartitionSpec as P

HEADS = 8
WC = 8
EPS = 1e-05
MESH = pl.DeviceIdType.MESH
BF16 = jnp.bfloat16
F32 = jnp.float32
NT = (((1,), (1,)), ((), ()))


def layer_norm(values, gain):
    mean = jnp.mean(values, axis=-1, keepdims=True)
    centred = values - mean
    spread = jnp.mean(centred * centred, axis=-1, keepdims=True)
    return centred * lax.rsqrt(spread + EPS) * gain


def merged(block):
    shards, rows, width = block.shape
    if rows % 16:
        return block.astype(F32).reshape(shards * rows, width).astype(BF16)
    return block.reshape(shards * rows, width)


def inner_factor(count):
    inner = 1
    while inner * inner * 4 <= count:
        inner *= 2
    return inner if count % inner == 0 else 1


class Sems:
    def __init__(self, ref=None):
        self.ref, self.used = ref, 0

    def take(self):
        self.used += 1
        return None if self.ref is None else self.ref.at[self.used - 1]


class Gather:
    def __init__(self, buf, geometry, x_first, sends, recvs):
        self.buf = buf
        self.geometry, self.x_first = geometry, x_first
        self.sends, self.recvs = sends, recvs
        self.pending = []
        self.late = []

    def rows(self, core):
        half = self.buf.shape[1] // 2
        return pl.ds(pl.multiple_of(core * half, half), half)

    def copy(self, first, count, core, target, sem_pair):
        piece = self.buf.at[pl.ds(first, count), self.rows(core)]
        return pltpu.make_async_remote_copy(
            src_ref=piece,
            dst_ref=piece,
            send_sem=sem_pair[0],
            recv_sem=sem_pair[1],
            device_id=target,
            device_id_type=MESH,
        )

    def pair(self):
        return self.sends.take(), self.recvs.take()

    def begin(self, copy, when=None):
        if when is None:
            copy.start()
        else:
            pl.when(when)(copy.start)
        self.pending.append((copy, when))

    def arrive(self, copy, when=None):
        if when is None:
            copy.wait_recv()
        else:
            pl.when(when)(copy.wait_recv)

    def share(self, first, count, when=None):
        g = self.geometry
        pair = self.pair()
        self.begin(self.copy(first, count, g["core"], g["partner"], pair), when)
        self.late.append((self.copy(first, count, 1 - g["core"], g["partner"], pair), when))

    def across(self, z, when=None):
        g = self.geometry
        inner, x, core = g["inner"], g["x"], g["core"]
        incoming = []
        for step in range(1, inner):
            pair = self.pair()
            to, source = lax.rem(x + step, inner), lax.rem(x + inner - step, inner)
            peer = g["at"](g["z"], to)
            self.begin(self.copy(z * inner + x, 1, core, peer, pair), when)
            incoming.append((z * inner + source, self.copy(z * inner + source, 1, core, peer, pair), when))
        return incoming

    def steps(self):
        g = self.geometry
        inner, outer, x, z, core = g["inner"], g["outer"], g["x"], g["z"], g["core"]
        width = inner if self.x_first else 1

        def first_of(at):
            return at * inner if self.x_first else at * inner + x

        if self.x_first:
            incoming = self.across(z)
            yield
            for _, copy, when in incoming:
                self.arrive(copy, when)
            for shard, _, when in incoming:
                self.share(shard, 1, when)
        crossing = []
        for step in range(outer):
            if step < outer - 1:
                right, left = self.pair(), self.pair()
                here_right = (z + 1 < outer) & (z - step >= 0)
                here_left = (z - 1 >= 0) & (z + step < outer)
                at_right, at_left = jnp.maximum(z - step, 0), jnp.minimum(z + step, outer - 1)
                up, down = jnp.minimum(z + 1, outer - 1), jnp.maximum(z - 1, 0)
                self.begin(self.copy(first_of(at_right), width, core, g["at"](up, x), right), here_right)
                self.begin(self.copy(first_of(at_left), width, core, g["at"](down, x), left), here_left)
            if step == 0:
                arrived = [(z, None)]
            for at, when in arrived:
                if not self.x_first:
                    crossing += self.across(at, when)
                if step:
                    self.share(first_of(at), width, when)
            if step == outer - 1:
                break
            yield
            from_left, from_right = z - 1 - step >= 0, z + 1 + step < outer
            at_left, at_right = jnp.maximum(z - 1 - step, 0), jnp.minimum(z + 1 + step, outer - 1)
            self.arrive(self.copy(first_of(at_left), width, core, g["at"](down, x), right), from_left)
            self.arrive(self.copy(first_of(at_right), width, core, g["at"](up, x), left), from_right)
            arrived = [(at_left, from_left), (at_right, from_right)]
        for shard, copy, when in crossing:
            yield
            self.arrive(copy, when)
            self.share(shard, 1, when)
        yield
        for copy, when in self.late:
            self.arrive(copy, when)

    def finish(self):
        for copy, when in self.pending:
            if when is None:
                copy.wait_send()
            else:
                pl.when(when)(copy.wait_send)


def window_block(state, gain_attn, gain_mlp, attn_ref, mlp_ref, sizes):
    n_qkv, n_up = sizes
    length, width = state.shape
    head_dim = width // HEADS
    normed = layer_norm(state, gain_attn).astype(BF16)
    w_qkv = merged(attn_ref[:, :n_qkv])
    qkv = lax.dot_general(normed, w_qkv, NT, preferred_element_type=F32).astype(BF16)
    query, key, value = (qkv[:, i * width : (i + 1) * width] for i in range(3))
    head = lax.broadcasted_iota(jnp.int32, (length, width), 1) // head_dim
    zero = jnp.zeros((), F32)
    wide = query.astype(F32)
    stacked = jnp.concatenate(
        [jnp.where(head == h, wide, zero).astype(BF16) for h in range(HEADS)], axis=0
    )
    scores = lax.dot_general(stacked, key, NT, preferred_element_type=F32) * head_dim ** (-0.5)
    scores = jnp.exp(scores - jnp.max(scores, axis=-1, keepdims=True))
    probs = (scores / jnp.sum(scores, axis=-1, keepdims=True)).astype(BF16)
    every = jnp.dot(probs, value, preferred_element_type=F32)
    mixed = jnp.zeros((length, width), F32)
    for h in range(HEADS):
        mixed = jnp.where(head == h, every[h * length : (h + 1) * length], mixed)
    w_proj = merged(attn_ref[:, n_qkv:])
    state = state + jnp.dot(mixed.astype(BF16), w_proj, preferred_element_type=F32)
    normed = layer_norm(state, gain_mlp).astype(BF16)
    w_up = merged(mlp_ref[:, :n_up])
    hidden = lax.dot_general(normed, w_up, NT, preferred_element_type=F32)
    hidden = jax.nn.gelu(hidden).astype(BF16)
    w_down = merged(mlp_ref[:, n_up:])
    return state + jnp.dot(hidden, w_down, preferred_element_type=F32)


def sem_count(outer, inner, x_first):
    moves = 2 * (outer - 1)
    if x_first:
        return 2 * (inner - 1) + 2 * moves
    return 2 * moves + (1 + moves) * (inner - 1) * 2


def kernel(
    groups, lons, inner, sizes,
    patches_hbm, embed_hbm, channel_embed, agg_query, gains, qkv_hbm, proj_hbm, up_hbm, down_hbm,
    out,
    patches, embed_weight, up_in, embedded, partial, aux_out, aux_in, mean_in, attn0, mlp0, attn1, mlp1, edge_out, edge_in, final_out, final_in,
    chunk_send, chunk_recv, own_sem, agg_send, agg_recv, aux_send, aux_recv, edge_send, edge_recv, fin_send, fin_recv, load_sem,
):
    chans, count, _ = patches.shape
    width = embed_weight.shape[2]
    owned = count // groups
    half = owned // 2
    me, lon = lax.axis_index("chan"), lax.axis_index("lon")
    west, east = lax.rem(lon + lons - 1, lons), lax.rem(lon + 1, lons)
    barrier = pltpu.get_barrier_semaphore()
    greeted = 0
    for step in range(1, lons):
        pl.semaphore_signal(barrier, inc=1, device_id=(me, lax.rem(lon + step, lons)), device_id_type=MESH)
        greeted += 1
    for step in range(1, groups):
        other = lax.rem(me + step, groups)
        for column in (lon, west, east):
            pl.semaphore_signal(barrier, inc=1, device_id=(other, column), device_id_type=MESH)
            greeted += 1

    n_qkv, n_proj, n_up, n_down = sizes
    n_attn = n_qkv + n_proj
    core = lax.rem(me, 2)
    outer = lons // inner
    geometry = {
        "inner": inner, "outer": outer, "core": core,
        "x": lax.rem(lon, inner), "z": lon // inner,
        "partner": (me + 1 - 2 * core, lon),
        "at": lambda z, x: (me, z * inner + x),
    }
    bufs = (attn0, mlp0, attn1, mlp1)
    own_copies = []
    for layer in range(2):
        attn, mlp = bufs[2 * layer].at[lon], bufs[2 * layer + 1].at[lon]
        moves = (
            (up_hbm.at[layer], up_in.at[layer]),
            (qkv_hbm.at[layer], attn.at[pl.ds(0, n_qkv)]),
            (proj_hbm.at[layer], attn.at[pl.ds(n_qkv, n_proj)]),
            (down_hbm.at[layer], mlp.at[pl.ds(n_up, n_down)]),
        )
        for at, (source, target) in enumerate(moves):
            copy = pltpu.make_async_copy(source, target, own_sem.at[4 * layer + at])
            copy.start()
            own_copies.append(copy)
    loads = [
        pltpu.make_async_copy(patches_hbm, patches, load_sem.at[0]),
        pltpu.make_async_copy(embed_hbm, embed_weight, load_sem.at[1]),
    ]
    for copy in loads:
        copy.start()
    for copy in own_copies:
        copy.wait()
    for layer in range(2):
        bufs[2 * layer + 1][lon, :n_up] = up_in[layer].T
    pl.semaphore_wait(barrier, greeted)

    offset, gathers = 0, []
    for at, order in enumerate((True, False, False, True)):
        pairs = sem_count(outer, inner, order)
        sends, recvs = Sems(chunk_send.at[pl.ds(offset, pairs)]), Sems(chunk_recv.at[pl.ds(offset, pairs)])
        gathers.append(Gather(bufs[at], geometry, order, sends, recvs))
        offset += pairs
    flows = [one.steps() for one in gathers]

    def advance(*which):
        for i in which:
            next(flows[i], None)

    def drain(*which):
        live = list(which)
        while live:
            for i in list(live):
                if next(flows[i], "end") == "end":
                    live.remove(i)

    advance(0, 1)

    for copy in loads:
        copy.wait()
    query = agg_query[...]
    scores = []
    for c in range(chans):
        value = jnp.dot(patches[c], embed_weight[c], preferred_element_type=F32)
        value = value + channel_embed[c : c + 1].astype(F32)
        embedded[c] = value
        scores.append(jnp.sum(value * query, axis=-1, keepdims=True) * width ** (-0.5))

    top = functools.reduce(jnp.maximum, scores)
    shares = [jnp.exp(score - top) for score in scores]
    denom = functools.reduce(jnp.add, shares)
    lane = lax.broadcasted_iota(jnp.int32, (count, 128), 1)
    aux = jnp.where(lane == 0, top, jnp.where(lane == 1, denom, 0.0))
    numer = shares[0] * embedded[0]
    for c in range(1, chans):
        numer = numer + shares[c] * embedded[c]
    mean = numer / denom
    for g in range(groups):
        partial[g] = mean[g * owned : (g + 1) * owned].astype(BF16)
        block = aux[g * owned : (g + 1) * owned]
        if owned < 128:
            block = jnp.concatenate([block, jnp.zeros((128 - owned, 128), F32)], axis=0)
        aux_out[g] = block.T[:8]
    sent = []
    for step in range(1, groups):
        to = lax.rem(me + step, groups)
        sent.append(
            pltpu.make_async_remote_copy(
                src_ref=partial.at[to], dst_ref=mean_in.at[step - 1],
                send_sem=agg_send.at[step - 1], recv_sem=agg_recv.at[step - 1],
                device_id=(to, lon), device_id_type=MESH,
            )
        )
        sent.append(
            pltpu.make_async_remote_copy(
                src_ref=aux_out.at[to], dst_ref=aux_in.at[step - 1],
                send_sem=aux_send.at[step - 1], recv_sem=aux_recv.at[step - 1],
                device_id=(to, lon), device_id_type=MESH,
            )
        )
    for copy in sent:
        copy.start()

    advance(0, 1, 2, 3)
    for _ in range(4):
        advance(0, 1, 2, 3)
    drain(0, 1)

    for copy in sent:
        copy.wait_recv()
    means = [partial[me].astype(F32)] + [mean_in[i].astype(F32) for i in range(groups - 1)]
    columns = [aux_out[me].T] + [aux_in[i].T for i in range(groups - 1)]
    tops = [column[:owned, 0:1] for column in columns]
    best = functools.reduce(jnp.maximum, tops)
    weights = [column[:owned, 1:2] * jnp.exp(one - best) for column, one in zip(columns, tops)]
    total = functools.reduce(jnp.add, weights)
    state = functools.reduce(jnp.add, [w * m for w, m in zip(weights, means)]) / total

    side = WC // 2

    def order_matrix(flip, kind):
        row = lax.broadcasted_iota(jnp.int32, (owned, owned), 1 if flip else 0)
        token = lax.broadcasted_iota(jnp.int32, (owned, owned), 0 if flip else 1)
        within = row % half
        return jnp.where((within // side) * WC + (row // half) * side + within % side == token, 1.0, 0.0).astype(kind)

    state = jnp.dot(order_matrix(False, F32), state, precision=lax.Precision.HIGHEST, preferred_element_type=F32)

    def gain(i):
        return gains[i : i + 1]

    state = window_block(state, gain(0), gain(1), attn0, mlp0, (n_qkv, n_up))
    edge_out[...] = state[:half].astype(BF16)
    edge = pltpu.make_async_remote_copy(
        src_ref=edge_out, dst_ref=edge_in, send_sem=edge_send.at[0], recv_sem=edge_recv.at[0],
        device_id=(me, west), device_id_type=MESH,
    )
    edge.start()
    drain(2, 3)
    edge.wait_recv()
    moved = jnp.concatenate([state[half:], edge_in[...].astype(F32)], axis=0)
    moved = window_block(moved, gain(2), gain(3), attn1, mlp1, (n_qkv, n_up))
    final = layer_norm(moved, gain(4)).astype(BF16)
    final_out[0] = final[half:]
    final_out[1] = final[:half]
    last = []
    for step in range(groups):
        to = lax.rem(me + step, groups)
        last.append(
            pltpu.make_async_remote_copy(
                src_ref=final_out.at[0], dst_ref=final_in.at[me, 0],
                send_sem=fin_send.at[step, 0], recv_sem=fin_recv.at[step, 0],
                device_id=(to, east), device_id_type=MESH,
            )
        )
        if step:
            last.append(
                pltpu.make_async_remote_copy(
                    src_ref=final_out.at[1], dst_ref=final_in.at[me, 1],
                    send_sem=fin_send.at[step, 1], recv_sem=fin_recv.at[step, 1],
                    device_id=(to, lon), device_id_type=MESH,
                )
            )
    for copy in last:
        copy.start()
    final_in[me, 1] = final[:half]
    arrivals = []
    for step in range(groups):
        source = lax.rem(me + groups - step, groups)
        for part in range(2):
            if step or part == 0:
                pltpu.make_async_remote_copy(
                    src_ref=final_out.at[part], dst_ref=final_in.at[source, part],
                    send_sem=fin_send.at[step, part], recv_sem=fin_recv.at[step, part],
                    device_id=(source, west if part == 0 else lon) if step else (me, west), device_id_type=MESH,
                ).wait_recv()
    back = order_matrix(True, BF16)
    for g in range(groups):
        out[g] = jnp.dot(back, merged(final_in[g]), preferred_element_type=F32).astype(BF16)

    for one in gathers:
        one.finish()
    for copy in sent + [edge] + last:
        copy.wait_send()


def body(
    patches, embed_weight, channel_embed, agg_query, norm_gains,
    qkv_weight, proj_weight, up_weight, down_weight, decode_weight,
):
    chans, rows, cols, width_p = patches.shape
    width = embed_weight.shape[2]
    count = rows * cols
    groups, lons = lax.axis_size("chan"), lax.axis_size("lon")
    owned = count // groups
    half = owned // 2
    assert cols == WC and owned <= 128
    sizes = (qkv_weight.shape[2], proj_weight.shape[1], up_weight.shape[2], down_weight.shape[1])
    n_attn, n_mlp = sizes[0] + sizes[1], sizes[2] + sizes[3]
    inner = inner_factor(lons)
    outer = lons // inner
    pairs = sum(sem_count(outer, inner, order) for order in (True, False, False, True))
    vmem = pl.BlockSpec(memory_space=pltpu.VMEM)
    hbm = pl.BlockSpec(memory_space=pl.ANY)
    tokens = pl.pallas_call(
        functools.partial(kernel, groups, lons, inner, sizes),
        out_shape=jax.ShapeDtypeStruct((groups, owned, width), BF16),
        in_specs=[hbm] * 2 + [vmem] * 3 + [hbm] * 4,
        out_specs=vmem,
        scratch_shapes=[
            pltpu.VMEM((chans, count, width_p), BF16),
            pltpu.VMEM(embed_weight.shape, BF16),
            pltpu.VMEM(up_weight.shape, BF16),
            pltpu.VMEM((chans, count, width), F32),
            pltpu.VMEM((groups, owned, width), BF16),
            pltpu.VMEM((groups, 8, 128), F32),
            pltpu.VMEM((groups - 1, 8, 128), F32),
            pltpu.VMEM((groups - 1, owned, width), BF16),
            pltpu.VMEM((lons, n_attn, width), BF16),
            pltpu.VMEM((lons, n_mlp, width), BF16),
            pltpu.VMEM((lons, n_attn, width), BF16),
            pltpu.VMEM((lons, n_mlp, width), BF16),
            pltpu.VMEM((half, width), BF16),
            pltpu.VMEM((half, width), BF16),
            pltpu.VMEM((2, half, width), BF16),
            pltpu.VMEM((groups, 2, half, width), BF16),
            pltpu.SemaphoreType.DMA((pairs,)),
            pltpu.SemaphoreType.DMA((pairs,)),
            pltpu.SemaphoreType.DMA((8,)),
            pltpu.SemaphoreType.DMA((groups - 1,)),
            pltpu.SemaphoreType.DMA((groups - 1,)),
            pltpu.SemaphoreType.DMA((groups - 1,)),
            pltpu.SemaphoreType.DMA((groups - 1,)),
            pltpu.SemaphoreType.DMA((1,)),
            pltpu.SemaphoreType.DMA((1,)),
            pltpu.SemaphoreType.DMA((groups, 2)),
            pltpu.SemaphoreType.DMA((groups, 2)),
            pltpu.SemaphoreType.DMA((2,)),
        ],
        compiler_params=pltpu.CompilerParams(
            collective_id=0, has_side_effects=True, vmem_limit_bytes=60 * 1024 * 1024
        ),
    )(
        patches.reshape(chans, count, width_p), embed_weight, channel_embed, agg_query.reshape(1, width),
        norm_gains, qkv_weight.transpose(0, 2, 1), proj_weight, up_weight, down_weight,
    )
    decoded = jnp.einsum(
        "te,cep->ctp", tokens.reshape(count, width), decode_weight, preferred_element_type=F32
    ).astype(BF16)
    return decoded.reshape(chans, rows, cols, -1)


def solution(mesh):
    placed = (
        P("chan", None, "lon", None),
        P("chan", None, None),
        P("chan", None),
        P(),
        P(),
        P(None, None, "lon"),
        P(None, "lon", None),
        P(None, None, "lon"),
        P(None, "lon", None),
        P("chan", None, None),
    )
    return jax.shard_map(
        body, mesh=mesh, in_specs=placed, out_specs=P("chan", None, "lon", None), check_vma=False
    )
```

```python
import functools

import jax
import jax.numpy as jnp
from jax import lax
from jax.experimental import pallas as pl
from jax.experimental.pallas import tpu as pltpu
from jax.sharding import PartitionSpec as P

HEADS = 8
WC = 8
EPS = 1e-05
MESH = pl.DeviceIdType.MESH
BF16 = jnp.bfloat16
F32 = jnp.float32
NT = (((1,), (1,)), ((), ()))


def layer_norm(values, gain):
    mean = jnp.mean(values, axis=-1, keepdims=True)
    centred = values - mean
    spread = jnp.mean(centred * centred, axis=-1, keepdims=True)
    return centred * lax.rsqrt(spread + EPS) * gain


def merged(block):
    shards, rows, width = block.shape
    if rows % 16:
        return block.astype(F32).reshape(shards * rows, width).astype(BF16)
    return block.reshape(shards * rows, width)


def inner_factor(count):
    inner = 1
    while inner * inner * 4 <= count:
        inner *= 2
    return inner if count % inner == 0 else 1


class Sems:
    def __init__(self, ref=None):
        self.ref, self.used = ref, 0

    def take(self):
        self.used += 1
        return None if self.ref is None else self.ref.at[self.used - 1]


class Gather:
    def __init__(self, buf, geometry, parts, sends, recvs):
        self.buf, self.geometry, self.parts = buf, geometry, parts
        self.sends, self.recvs = sends, recvs
        self.pending, self.late, self.inbox = [], [], []

    def copy(self, shard, part, target, sem_pair):
        size = self.buf.shape[1] // self.parts
        piece = self.buf.at[shard, pl.ds(pl.multiple_of(part * size, size), size)]
        return pltpu.make_async_remote_copy(
            src_ref=piece,
            dst_ref=piece,
            send_sem=sem_pair[0],
            recv_sem=sem_pair[1],
            device_id=target,
            device_id_type=MESH,
        )

    def begin(self, copy, when):
        if when is None:
            copy.start()
        else:
            pl.when(when)(copy.start)
        self.pending.append((copy, when))

    def arrive(self, copy, when):
        if when is None:
            copy.wait_recv()
        else:
            pl.when(when)(copy.wait_recv)

    def exchange(self, shard, part, shard_in, part_in, peer, when, when_in, then):
        pair = self.sends.take(), self.recvs.take()
        self.begin(self.copy(shard, part, peer, pair), when)
        arrival = self.copy(shard_in, part_in, peer, pair)
        if then is None:
            self.late.append((arrival, when_in))
        else:
            self.inbox.append((arrival, when_in, then))

    def mine(self):
        return self.geometry["part"](self.parts)

    def to_core(self, shard, part, when):
        g = self.geometry
        other = part + 1 - 2 * g["core"]
        self.exchange(shard, part, shard, other, g["partner"], when, when, None)

    def share(self, shard, when):
        g, part = self.geometry, self.mine()
        self.to_core(shard, part, when)
        if self.parts == 4:
            other = lax.rem(part + 2, 4)
            self.exchange(
                shard, part, shard, other, g["across"], when, when, lambda: self.to_core(shard, other, when)
            )

    def to_x(self, z, when):
        g = self.geometry
        inner, x = g["inner"], g["x"]
        for step in range(1, inner):
            to, source = lax.rem(x + step, inner), lax.rem(x + inner - step, inner)
            shard = z * inner + source
            self.exchange(
                z * inner + x, self.mine(), shard, self.mine(), g["at"](g["z"], to), when, when,
                functools.partial(self.share, shard, when),
            )

    def to_z(self, step, way):
        g = self.geometry
        inner, outer, x, z = g["inner"], g["outer"], g["x"], g["z"]
        if step >= outer - 1:
            return
        part = self.mine()

        def inside(at):
            return (at >= 0) & (at < outer), jnp.clip(at, 0, outer - 1)

        has_next, after = inside(z + way)
        has_out, out = inside(z - way * step)
        has_in, source = inside(z - way * (step + 1))

        def then():
            self.to_z(step + 1, way)
            self.to_x(source, has_in)
            self.share(source * inner + x, has_in)

        self.exchange(
            out * inner + x, part, source * inner + x, part, g["at"](after, x), has_next & has_out, has_in, then
        )

    def steps(self):
        self.to_z(0, 1)
        self.to_z(0, -1)
        self.to_x(self.geometry["z"], None)
        yield
        while self.inbox:
            now, self.inbox = self.inbox, []
            for copy, when, then in now:
                self.arrive(copy, when)
                then()
            yield
        for copy, when in self.late:
            self.arrive(copy, when)

    def finish(self):
        for copy, when in self.pending:
            if when is None:
                copy.wait_send()
            else:
                pl.when(when)(copy.wait_send)


def sem_count(outer, inner, parts):
    lines = 2 * (outer - 1)
    crosses = (1 + lines) * (inner - 1)
    return lines + crosses + (lines + crosses) * (1 if parts == 2 else 3)


def window_block(state, gain_attn, gain_mlp, attn_ref, mlp_ref, sizes, ready_mlp):
    n_qkv, n_up = sizes
    length, width = state.shape
    head_dim = width // HEADS
    normed = layer_norm(state, gain_attn).astype(BF16)
    w_qkv = merged(attn_ref[:, :n_qkv])
    qkv = lax.dot_general(normed, w_qkv, NT, preferred_element_type=F32).astype(BF16)
    query, key, value = (qkv[:, i * width : (i + 1) * width] for i in range(3))
    head = lax.broadcasted_iota(jnp.int32, (length, width), 1) // head_dim
    zero = jnp.zeros((), F32)
    wide = query.astype(F32)
    stacked = jnp.concatenate(
        [jnp.where(head == h, wide, zero).astype(BF16) for h in range(HEADS)], axis=0
    )
    scores = lax.dot_general(stacked, key, NT, preferred_element_type=F32) * head_dim ** (-0.5)
    scores = jnp.exp(scores - jnp.max(scores, axis=-1, keepdims=True))
    probs = (scores / jnp.sum(scores, axis=-1, keepdims=True)).astype(BF16)
    every = jnp.dot(probs, value, preferred_element_type=F32)
    mixed = jnp.zeros((length, width), F32)
    for h in range(HEADS):
        mixed = jnp.where(head == h, every[h * length : (h + 1) * length], mixed)
    w_proj = merged(attn_ref[:, n_qkv:])
    state = state + jnp.dot(mixed.astype(BF16), w_proj, preferred_element_type=F32)
    normed = layer_norm(state, gain_mlp).astype(BF16)
    ready_mlp()
    w_up = merged(mlp_ref[:, :n_up])
    hidden = lax.dot_general(normed, w_up, NT, preferred_element_type=F32)
    hidden = jax.nn.gelu(hidden).astype(BF16)
    w_down = merged(mlp_ref[:, n_up:])
    return state + jnp.dot(hidden, w_down, preferred_element_type=F32)


def chunk_parts(groups):
    return (2, 4, 2, 4) if groups % 4 == 0 else (2, 2, 2, 2)


def kernel(
    groups, lons, inner, sizes,
    patches_hbm, embed_hbm, channel_embed, agg_query, gains, qkv_hbm, proj_hbm, up_hbm, down_hbm,
    out,
    patches, embed_weight, up_in, embedded, partial, aux_out, aux_in, mean_in, attn0, mlp0, attn1, mlp1, edge_out, edge_in, final_out, final_in,
    chunk_send, chunk_recv, own_sem, agg_send, agg_recv, aux_send, aux_recv, edge_send, edge_recv, fin_send, fin_recv, load_sem,
):
    chans, count, _ = patches.shape
    width = embed_weight.shape[2]
    owned = count // groups
    half = owned // 2
    me, lon = lax.axis_index("chan"), lax.axis_index("lon")
    west, east = lax.rem(lon + lons - 1, lons), lax.rem(lon + 1, lons)
    barrier = pltpu.get_barrier_semaphore()
    greeted = 0
    for step in range(1, lons):
        pl.semaphore_signal(barrier, inc=1, device_id=(me, lax.rem(lon + step, lons)), device_id_type=MESH)
        greeted += 1
    for step in range(1, groups):
        other = lax.rem(me + step, groups)
        for column in (lon, west, east):
            pl.semaphore_signal(barrier, inc=1, device_id=(other, column), device_id_type=MESH)
            greeted += 1

    n_qkv, n_proj, n_up, n_down = sizes
    n_attn = n_qkv + n_proj
    core = lax.rem(me, 2)
    outer = lons // inner
    geometry = {
        "inner": inner, "outer": outer, "core": core,
        "x": lax.rem(lon, inner), "z": lon // inner,
        "partner": (me + 1 - 2 * core, lon),
        "across": (me + 2 - 4 * (lax.rem(me, 4) // 2), lon),
        "part": lambda parts: lax.rem(me, parts),
        "at": lambda z, x: (me, z * inner + x),
    }
    bufs = (attn0, mlp0, attn1, mlp1)
    own_copies = []
    for layer in range(2):
        attn, mlp = bufs[2 * layer].at[lon], bufs[2 * layer + 1].at[lon]
        moves = (
            (up_hbm.at[layer], up_in.at[layer]),
            (qkv_hbm.at[layer], attn.at[pl.ds(0, n_qkv)]),
            (proj_hbm.at[layer], attn.at[pl.ds(n_qkv, n_proj)]),
            (down_hbm.at[layer], mlp.at[pl.ds(n_up, n_down)]),
        )
        for at, (source, target) in enumerate(moves):
            copy = pltpu.make_async_copy(source, target, own_sem.at[4 * layer + at])
            copy.start()
            own_copies.append(copy)
    loads = [
        pltpu.make_async_copy(patches_hbm, patches, load_sem.at[0]),
        pltpu.make_async_copy(embed_hbm, embed_weight, load_sem.at[1]),
    ]
    for copy in loads:
        copy.start()
    for copy in own_copies:
        copy.wait()
    for layer in range(2):
        bufs[2 * layer + 1][lon, :n_up] = up_in[layer].T
    pl.semaphore_wait(barrier, greeted)

    offset, gathers = 0, []
    for at, parts in enumerate(chunk_parts(groups)):
        pairs = sem_count(outer, inner, parts)
        sends, recvs = Sems(chunk_send.at[pl.ds(offset, pairs)]), Sems(chunk_recv.at[pl.ds(offset, pairs)])
        gathers.append(Gather(bufs[at], geometry, parts, sends, recvs))
        offset += pairs
    flows = [one.steps() for one in gathers]

    def advance(*which):
        for i in which:
            next(flows[i], None)

    def drain(*which):
        live = list(which)
        while live:
            for i in list(live):
                if next(flows[i], "end") == "end":
                    live.remove(i)

    advance(0, 1)

    for copy in loads:
        copy.wait()
    query = agg_query[...]
    scores = []
    for c in range(chans):
        value = jnp.dot(patches[c], embed_weight[c], preferred_element_type=F32)
        value = value + channel_embed[c : c + 1].astype(F32)
        embedded[c] = value
        scores.append(jnp.sum(value * query, axis=-1, keepdims=True) * width ** (-0.5))

    top = functools.reduce(jnp.maximum, scores)
    shares = [jnp.exp(score - top) for score in scores]
    denom = functools.reduce(jnp.add, shares)
    lane = lax.broadcasted_iota(jnp.int32, (count, 128), 1)
    aux = jnp.where(lane == 0, top, jnp.where(lane == 1, denom, 0.0))
    numer = shares[0] * embedded[0]
    for c in range(1, chans):
        numer = numer + shares[c] * embedded[c]
    mean = numer / denom
    for g in range(groups):
        partial[g] = mean[g * owned : (g + 1) * owned].astype(BF16)
        block = aux[g * owned : (g + 1) * owned]
        if owned < 128:
            block = jnp.concatenate([block, jnp.zeros((128 - owned, 128), F32)], axis=0)
        aux_out[g] = block.T[:8]
    sent = []
    for step in range(1, groups):
        to = lax.rem(me + step, groups)
        sent.append(
            pltpu.make_async_remote_copy(
                src_ref=partial.at[to], dst_ref=mean_in.at[step - 1],
                send_sem=agg_send.at[step - 1], recv_sem=agg_recv.at[step - 1],
                device_id=(to, lon), device_id_type=MESH,
            )
        )
        sent.append(
            pltpu.make_async_remote_copy(
                src_ref=aux_out.at[to], dst_ref=aux_in.at[step - 1],
                send_sem=aux_send.at[step - 1], recv_sem=aux_recv.at[step - 1],
                device_id=(to, lon), device_id_type=MESH,
            )
        )
    for copy in sent:
        copy.start()

    advance(0, 1)
    advance(0, 1)
    advance(2, 3)
    advance(0, 1)
    advance(0, 1)
    advance(2, 3)
    drain(0)

    for copy in sent:
        copy.wait_recv()
    means = [partial[me].astype(F32)] + [mean_in[i].astype(F32) for i in range(groups - 1)]
    columns = [aux_out[me].T] + [aux_in[i].T for i in range(groups - 1)]
    tops = [column[:owned, 0:1] for column in columns]
    best = functools.reduce(jnp.maximum, tops)
    weights = [column[:owned, 1:2] * jnp.exp(one - best) for column, one in zip(columns, tops)]
    total = functools.reduce(jnp.add, weights)
    state = functools.reduce(jnp.add, [w * m for w, m in zip(weights, means)]) / total

    side = WC // 2

    def order_matrix(flip, kind):
        row = lax.broadcasted_iota(jnp.int32, (owned, owned), 1 if flip else 0)
        token = lax.broadcasted_iota(jnp.int32, (owned, owned), 0 if flip else 1)
        within = row % half
        return jnp.where((within // side) * WC + (row // half) * side + within % side == token, 1.0, 0.0).astype(kind)

    state = jnp.dot(order_matrix(False, F32), state, precision=lax.Precision.HIGHEST, preferred_element_type=F32)

    def gain(i):
        return gains[i : i + 1]

    state = window_block(state, gain(0), gain(1), attn0, mlp0, (n_qkv, n_up), lambda: drain(1))
    edge_out[...] = state[:half].astype(BF16)
    edge = pltpu.make_async_remote_copy(
        src_ref=edge_out, dst_ref=edge_in, send_sem=edge_send.at[0], recv_sem=edge_recv.at[0],
        device_id=(me, west), device_id_type=MESH,
    )
    edge.start()
    for _ in range(4):
        advance(2, 3)
    drain(2)
    edge.wait_recv()
    moved = jnp.concatenate([state[half:], edge_in[...].astype(F32)], axis=0)
    moved = window_block(moved, gain(2), gain(3), attn1, mlp1, (n_qkv, n_up), lambda: drain(3))
    final = layer_norm(moved, gain(4)).astype(BF16)
    final_out[0] = final[half:]
    final_out[1] = final[:half]
    last = []
    for step in range(groups):
        to = lax.rem(me + step, groups)
        last.append(
            pltpu.make_async_remote_copy(
                src_ref=final_out.at[0], dst_ref=final_in.at[me, 0],
                send_sem=fin_send.at[step, 0], recv_sem=fin_recv.at[step, 0],
                device_id=(to, east), device_id_type=MESH,
            )
        )
        if step:
            last.append(
                pltpu.make_async_remote_copy(
                    src_ref=final_out.at[1], dst_ref=final_in.at[me, 1],
                    send_sem=fin_send.at[step, 1], recv_sem=fin_recv.at[step, 1],
                    device_id=(to, lon), device_id_type=MESH,
                )
            )
    for copy in last:
        copy.start()
    final_in[me, 1] = final[:half]
    arrivals = []
    for step in range(groups):
        source = lax.rem(me + groups - step, groups)
        for part in range(2):
            if step or part == 0:
                pltpu.make_async_remote_copy(
                    src_ref=final_out.at[part], dst_ref=final_in.at[source, part],
                    send_sem=fin_send.at[step, part], recv_sem=fin_recv.at[step, part],
                    device_id=(source, west if part == 0 else lon) if step else (me, west), device_id_type=MESH,
                ).wait_recv()
    back = order_matrix(True, BF16)
    for g in range(groups):
        out[g] = jnp.dot(back, merged(final_in[g]), preferred_element_type=F32).astype(BF16)

    for one in gathers:
        one.finish()
    for copy in sent + [edge] + last:
        copy.wait_send()


def body(
    patches, embed_weight, channel_embed, agg_query, norm_gains,
    qkv_weight, proj_weight, up_weight, down_weight, decode_weight,
):
    chans, rows, cols, width_p = patches.shape
    width = embed_weight.shape[2]
    count = rows * cols
    groups, lons = lax.axis_size("chan"), lax.axis_size("lon")
    owned = count // groups
    half = owned // 2
    assert cols == WC and owned <= 128
    sizes = (qkv_weight.shape[2], proj_weight.shape[1], up_weight.shape[2], down_weight.shape[1])
    n_attn, n_mlp = sizes[0] + sizes[1], sizes[2] + sizes[3]
    inner = inner_factor(lons)
    outer = lons // inner
    pairs = sum(sem_count(outer, inner, parts) for parts in chunk_parts(groups))
    vmem = pl.BlockSpec(memory_space=pltpu.VMEM)
    hbm = pl.BlockSpec(memory_space=pl.ANY)
    tokens = pl.pallas_call(
        functools.partial(kernel, groups, lons, inner, sizes),
        out_shape=jax.ShapeDtypeStruct((groups, owned, width), BF16),
        in_specs=[hbm] * 2 + [vmem] * 3 + [hbm] * 4,
        out_specs=vmem,
        scratch_shapes=[
            pltpu.VMEM((chans, count, width_p), BF16),
            pltpu.VMEM(embed_weight.shape, BF16),
            pltpu.VMEM(up_weight.shape, BF16),
            pltpu.VMEM((chans, count, width), F32),
            pltpu.VMEM((groups, owned, width), BF16),
            pltpu.VMEM((groups, 8, 128), F32),
            pltpu.VMEM((groups - 1, 8, 128), F32),
            pltpu.VMEM((groups - 1, owned, width), BF16),
            pltpu.VMEM((lons, n_attn, width), BF16),
            pltpu.VMEM((lons, n_mlp, width), BF16),
            pltpu.VMEM((lons, n_attn, width), BF16),
            pltpu.VMEM((lons, n_mlp, width), BF16),
            pltpu.VMEM((half, width), BF16),
            pltpu.VMEM((half, width), BF16),
            pltpu.VMEM((2, half, width), BF16),
            pltpu.VMEM((groups, 2, half, width), BF16),
            pltpu.SemaphoreType.DMA((pairs,)),
            pltpu.SemaphoreType.DMA((pairs,)),
            pltpu.SemaphoreType.DMA((8,)),
            pltpu.SemaphoreType.DMA((groups - 1,)),
            pltpu.SemaphoreType.DMA((groups - 1,)),
            pltpu.SemaphoreType.DMA((groups - 1,)),
            pltpu.SemaphoreType.DMA((groups - 1,)),
            pltpu.SemaphoreType.DMA((1,)),
            pltpu.SemaphoreType.DMA((1,)),
            pltpu.SemaphoreType.DMA((groups, 2)),
            pltpu.SemaphoreType.DMA((groups, 2)),
            pltpu.SemaphoreType.DMA((2,)),
        ],
        compiler_params=pltpu.CompilerParams(
            collective_id=0, has_side_effects=True, vmem_limit_bytes=60 * 1024 * 1024
        ),
    )(
        patches.reshape(chans, count, width_p), embed_weight, channel_embed, agg_query.reshape(1, width),
        norm_gains, qkv_weight.transpose(0, 2, 1), proj_weight, up_weight, down_weight,
    )
    decoded = jnp.einsum(
        "te,cep->ctp", tokens.reshape(count, width), decode_weight, preferred_element_type=F32
    ).astype(BF16)
    return decoded.reshape(chans, rows, cols, -1)


def solution(mesh):
    placed = (
        P("chan", None, "lon", None),
        P("chan", None, None),
        P("chan", None),
        P(),
        P(),
        P(None, None, "lon"),
        P(None, "lon", None),
        P(None, None, "lon"),
        P(None, "lon", None),
        P("chan", None, None),
    )
    return jax.shard_map(
        body, mesh=mesh, in_specs=placed, out_specs=P("chan", None, "lon", None), check_vma=False
    )
```

```python
import functools

import jax
import jax.numpy as jnp
from jax import lax
from jax.experimental import pallas as pl
from jax.experimental.pallas import tpu as pltpu
from jax.sharding import PartitionSpec as P

HEADS = 8
WC = 8
EPS = 1e-05
MESH = pl.DeviceIdType.MESH
BF16 = jnp.bfloat16
F32 = jnp.float32
NT = (((1,), (1,)), ((), ()))


def layer_norm(values, gain):
    mean = jnp.mean(values, axis=-1, keepdims=True)
    centred = values - mean
    spread = jnp.mean(centred * centred, axis=-1, keepdims=True)
    return centred * lax.rsqrt(spread + EPS) * gain


def merged(block):
    shards, rows, width = block.shape
    if rows % 16:
        return block.astype(F32).reshape(shards * rows, width).astype(BF16)
    return block.reshape(shards * rows, width)


def inner_factor(count):
    inner = 1
    while inner * inner * 4 <= count:
        inner *= 2
    return inner if count % inner == 0 else 1


class Sems:
    def __init__(self, ref=None):
        self.ref, self.used = ref, 0

    def take(self):
        self.used += 1
        return None if self.ref is None else self.ref.at[self.used - 1]


class Gather:
    def __init__(self, buf, geometry, parts, sends, recvs):
        self.buf, self.geometry, self.parts = buf, geometry, parts
        self.sends, self.recvs = sends, recvs
        self.pending, self.late, self.inbox = [], [], []

    def copy(self, shard, part, target, sem_pair):
        size = self.buf.shape[1] // self.parts
        piece = self.buf.at[shard, pl.ds(pl.multiple_of(part * size, size), size)]
        return pltpu.make_async_remote_copy(
            src_ref=piece,
            dst_ref=piece,
            send_sem=sem_pair[0],
            recv_sem=sem_pair[1],
            device_id=target,
            device_id_type=MESH,
        )

    def exchange(self, shard, part, shard_in, part_in, peer, then):
        pair = self.sends.take(), self.recvs.take()
        copy = self.copy(shard, part, peer, pair)
        copy.start()
        self.pending.append(copy)
        arrival = self.copy(shard_in, part_in, peer, pair)
        if then is None:
            self.late.append(arrival)
        else:
            self.inbox.append((arrival, then))

    def mine(self):
        return self.geometry["part"](self.parts)

    def to_core(self, shard, part):
        g = self.geometry
        self.exchange(shard, part, shard, part + 1 - 2 * g["core"], g["partner"], None)

    def share(self, shard):
        g, part = self.geometry, self.mine()
        if self.parts == 4:
            other = lax.rem(part + 2, 4)
            self.exchange(shard, part, shard, other, g["across"], lambda: self.to_core(shard, other))
        self.to_core(shard, part)

    def to_x(self, z):
        g = self.geometry
        inner, x = g["inner"], g["x"]
        for step in range(1, inner):
            to, source = lax.rem(x + step, inner), lax.rem(x + inner - step, inner)
            shard = z * inner + source
            self.exchange(
                z * inner + x, self.mine(), shard, self.mine(), g["at"](g["z"], to),
                functools.partial(self.share, shard),
            )

    def to_z(self):
        g = self.geometry
        inner, outer, x, z = g["inner"], g["outer"], g["x"], g["z"]
        for step in range(1, outer):
            to, source = lax.rem(z + step, outer), lax.rem(z + outer - step, outer)
            shard = source * inner + x

            def then(source=source, shard=shard):
                self.to_x(source)
                self.share(shard)

            self.exchange(z * inner + x, self.mine(), shard, self.mine(), g["at"](to, x), then)

    def steps(self):
        self.to_z()
        self.to_x(self.geometry["z"])
        yield
        while self.inbox:
            now, self.inbox = self.inbox, []
            for copy, then in now:
                copy.wait_recv()
                then()
            yield
        for copy in self.late:
            copy.wait_recv()

    def finish(self):
        for copy in self.pending:
            copy.wait_send()


def sem_count(outer, inner, parts):
    lines = outer - 1
    crosses = (1 + lines) * (inner - 1)
    return lines + crosses + (lines + crosses) * (1 if parts == 2 else 3)


def window_block(state, gain_attn, gain_mlp, attn_ref, mlp_ref, sizes, ready_mlp):
    n_qkv, n_up = sizes
    length, width = state.shape
    head_dim = width // HEADS
    normed = layer_norm(state, gain_attn).astype(BF16)
    w_qkv = merged(attn_ref[:, :n_qkv])
    qkv = lax.dot_general(normed, w_qkv, NT, preferred_element_type=F32).astype(BF16)
    query, key, value = (qkv[:, i * width : (i + 1) * width] for i in range(3))
    head = lax.broadcasted_iota(jnp.int32, (length, width), 1) // head_dim
    zero = jnp.zeros((), F32)
    wide = query.astype(F32)
    stacked = jnp.concatenate(
        [jnp.where(head == h, wide, zero).astype(BF16) for h in range(HEADS)], axis=0
    )
    scores = lax.dot_general(stacked, key, NT, preferred_element_type=F32) * head_dim ** (-0.5)
    scores = jnp.exp(scores - jnp.max(scores, axis=-1, keepdims=True))
    probs = (scores / jnp.sum(scores, axis=-1, keepdims=True)).astype(BF16)
    every = jnp.dot(probs, value, preferred_element_type=F32)
    mixed = jnp.zeros((length, width), F32)
    for h in range(HEADS):
        mixed = jnp.where(head == h, every[h * length : (h + 1) * length], mixed)
    w_proj = merged(attn_ref[:, n_qkv:])
    state = state + jnp.dot(mixed.astype(BF16), w_proj, preferred_element_type=F32)
    normed = layer_norm(state, gain_mlp).astype(BF16)
    ready_mlp()
    w_up = merged(mlp_ref[:, :n_up])
    hidden = lax.dot_general(normed, w_up, NT, preferred_element_type=F32)
    hidden = jax.nn.gelu(hidden).astype(BF16)
    w_down = merged(mlp_ref[:, n_up:])
    return state + jnp.dot(hidden, w_down, preferred_element_type=F32)


def chunk_parts(groups):
    return (2, 4, 2, 4) if groups % 4 == 0 else (2, 2, 2, 2)


def kernel(
    groups, lons, inner, sizes,
    patches_hbm, embed_hbm, channel_embed, agg_query, gains, qkv_hbm, proj_hbm, up_hbm, down_hbm,
    out,
    patches, embed_weight, up_in, embedded, partial, aux_out, aux_in, mean_in, attn0, mlp0, attn1, mlp1, edge_out, edge_in, final_out, final_in,
    chunk_send, chunk_recv, own_sem, agg_send, agg_recv, aux_send, aux_recv, edge_send, edge_recv, fin_send, fin_recv, load_sem,
):
    chans, count, _ = patches.shape
    width = embed_weight.shape[2]
    owned = count // groups
    half = owned // 2
    me, lon = lax.axis_index("chan"), lax.axis_index("lon")
    west, east = lax.rem(lon + lons - 1, lons), lax.rem(lon + 1, lons)
    barrier = pltpu.get_barrier_semaphore()
    greeted = 0
    for step in range(1, lons):
        pl.semaphore_signal(barrier, inc=1, device_id=(me, lax.rem(lon + step, lons)), device_id_type=MESH)
        greeted += 1
    for step in range(1, groups):
        other = lax.rem(me + step, groups)
        for column in (lon, west, east):
            pl.semaphore_signal(barrier, inc=1, device_id=(other, column), device_id_type=MESH)
            greeted += 1

    n_qkv, n_proj, n_up, n_down = sizes
    n_attn = n_qkv + n_proj
    core = lax.rem(me, 2)
    outer = lons // inner
    geometry = {
        "inner": inner, "outer": outer, "core": core,
        "x": lax.rem(lon, inner), "z": lon // inner,
        "partner": (me + 1 - 2 * core, lon),
        "across": (me + 2 - 4 * (lax.rem(me, 4) // 2), lon),
        "part": lambda parts: lax.rem(me, parts),
        "at": lambda z, x: (me, z * inner + x),
    }
    bufs = (attn0, mlp0, attn1, mlp1)
    own_copies = []
    for layer in range(2):
        attn, mlp = bufs[2 * layer].at[lon], bufs[2 * layer + 1].at[lon]
        moves = (
            (up_hbm.at[layer], up_in.at[layer]),
            (qkv_hbm.at[layer], attn.at[pl.ds(0, n_qkv)]),
            (proj_hbm.at[layer], attn.at[pl.ds(n_qkv, n_proj)]),
            (down_hbm.at[layer], mlp.at[pl.ds(n_up, n_down)]),
        )
        for at, (source, target) in enumerate(moves):
            copy = pltpu.make_async_copy(source, target, own_sem.at[4 * layer + at])
            copy.start()
            own_copies.append(copy)
    loads = [
        pltpu.make_async_copy(patches_hbm, patches, load_sem.at[0]),
        pltpu.make_async_copy(embed_hbm, embed_weight, load_sem.at[1]),
    ]
    for copy in loads:
        copy.start()
    for copy in own_copies:
        copy.wait()
    for layer in range(2):
        bufs[2 * layer + 1][lon, :n_up] = up_in[layer].T
    pl.semaphore_wait(barrier, greeted)

    offset, gathers = 0, []
    for at, parts in enumerate(chunk_parts(groups)):
        pairs = sem_count(outer, inner, parts)
        sends, recvs = Sems(chunk_send.at[pl.ds(offset, pairs)]), Sems(chunk_recv.at[pl.ds(offset, pairs)])
        gathers.append(Gather(bufs[at], geometry, parts, sends, recvs))
        offset += pairs
    flows = [one.steps() for one in gathers]

    def advance(*which):
        for i in which:
            next(flows[i], None)

    def drain(*which):
        live = list(which)
        while live:
            for i in list(live):
                if next(flows[i], "end") == "end":
                    live.remove(i)

    advance(0, 1)

    for copy in loads:
        copy.wait()
    query = agg_query[...]
    scores = []
    for c in range(chans):
        value = jnp.dot(patches[c], embed_weight[c], preferred_element_type=F32)
        value = value + channel_embed[c : c + 1].astype(F32)
        embedded[c] = value
        scores.append(jnp.sum(value * query, axis=-1, keepdims=True) * width ** (-0.5))

    top = functools.reduce(jnp.maximum, scores)
    shares = [jnp.exp(score - top) for score in scores]
    denom = functools.reduce(jnp.add, shares)
    lane = lax.broadcasted_iota(jnp.int32, (count, 128), 1)
    aux = jnp.where(lane == 0, top, jnp.where(lane == 1, denom, 0.0))
    numer = shares[0] * embedded[0]
    for c in range(1, chans):
        numer = numer + shares[c] * embedded[c]
    mean = numer / denom
    for g in range(groups):
        partial[g] = mean[g * owned : (g + 1) * owned].astype(BF16)
        block = aux[g * owned : (g + 1) * owned]
        if owned < 128:
            block = jnp.concatenate([block, jnp.zeros((128 - owned, 128), F32)], axis=0)
        aux_out[g] = block.T[:8]
    sent = []
    for step in range(1, groups):
        to = lax.rem(me + step, groups)
        sent.append(
            pltpu.make_async_remote_copy(
                src_ref=partial.at[to], dst_ref=mean_in.at[step - 1],
                send_sem=agg_send.at[step - 1], recv_sem=agg_recv.at[step - 1],
                device_id=(to, lon), device_id_type=MESH,
            )
        )
        sent.append(
            pltpu.make_async_remote_copy(
                src_ref=aux_out.at[to], dst_ref=aux_in.at[step - 1],
                send_sem=aux_send.at[step - 1], recv_sem=aux_recv.at[step - 1],
                device_id=(to, lon), device_id_type=MESH,
            )
        )
    for copy in sent:
        copy.start()

    advance(0, 1)
    advance(2, 3)
    advance(0, 1)
    advance(2, 3)
    advance(1)
    drain(0)

    for copy in sent:
        copy.wait_recv()
    means = [partial[me].astype(F32)] + [mean_in[i].astype(F32) for i in range(groups - 1)]
    columns = [aux_out[me].T] + [aux_in[i].T for i in range(groups - 1)]
    tops = [column[:owned, 0:1] for column in columns]
    best = functools.reduce(jnp.maximum, tops)
    weights = [column[:owned, 1:2] * jnp.exp(one - best) for column, one in zip(columns, tops)]
    total = functools.reduce(jnp.add, weights)
    state = functools.reduce(jnp.add, [w * m for w, m in zip(weights, means)]) / total

    side = WC // 2

    def order_matrix(flip, kind):
        row = lax.broadcasted_iota(jnp.int32, (owned, owned), 1 if flip else 0)
        token = lax.broadcasted_iota(jnp.int32, (owned, owned), 0 if flip else 1)
        within = row % half
        return jnp.where((within // side) * WC + (row // half) * side + within % side == token, 1.0, 0.0).astype(kind)

    state = jnp.dot(order_matrix(False, F32), state, precision=lax.Precision.HIGHEST, preferred_element_type=F32)

    def gain(i):
        return gains[i : i + 1]

    state = window_block(state, gain(0), gain(1), attn0, mlp0, (n_qkv, n_up), lambda: drain(1))
    edge_out[...] = state[:half].astype(BF16)
    edge = pltpu.make_async_remote_copy(
        src_ref=edge_out, dst_ref=edge_in, send_sem=edge_send.at[0], recv_sem=edge_recv.at[0],
        device_id=(me, west), device_id_type=MESH,
    )
    edge.start()
    advance(2, 3)
    advance(3)
    drain(2)
    edge.wait_recv()
    moved = jnp.concatenate([state[half:], edge_in[...].astype(F32)], axis=0)
    moved = window_block(moved, gain(2), gain(3), attn1, mlp1, (n_qkv, n_up), lambda: drain(3))
    final = layer_norm(moved, gain(4)).astype(BF16)
    final_out[0] = final[half:]
    final_out[1] = final[:half]
    last = []
    for step in range(groups):
        to = lax.rem(me + step, groups)
        last.append(
            pltpu.make_async_remote_copy(
                src_ref=final_out.at[0], dst_ref=final_in.at[me, 0],
                send_sem=fin_send.at[step, 0], recv_sem=fin_recv.at[step, 0],
                device_id=(to, east), device_id_type=MESH,
            )
        )
        if step:
            last.append(
                pltpu.make_async_remote_copy(
                    src_ref=final_out.at[1], dst_ref=final_in.at[me, 1],
                    send_sem=fin_send.at[step, 1], recv_sem=fin_recv.at[step, 1],
                    device_id=(to, lon), device_id_type=MESH,
                )
            )
    for copy in last:
        copy.start()
    final_in[me, 1] = final[:half]
    arrivals = []
    for step in range(groups):
        source = lax.rem(me + groups - step, groups)
        for part in range(2):
            if step or part == 0:
                pltpu.make_async_remote_copy(
                    src_ref=final_out.at[part], dst_ref=final_in.at[source, part],
                    send_sem=fin_send.at[step, part], recv_sem=fin_recv.at[step, part],
                    device_id=(source, west if part == 0 else lon) if step else (me, west), device_id_type=MESH,
                ).wait_recv()
    back = order_matrix(True, BF16)
    for g in range(groups):
        out[g] = jnp.dot(back, merged(final_in[g]), preferred_element_type=F32).astype(BF16)

    for one in gathers:
        one.finish()
    for copy in sent + [edge] + last:
        copy.wait_send()


def body(
    patches, embed_weight, channel_embed, agg_query, norm_gains,
    qkv_weight, proj_weight, up_weight, down_weight, decode_weight,
):
    chans, rows, cols, width_p = patches.shape
    width = embed_weight.shape[2]
    count = rows * cols
    groups, lons = lax.axis_size("chan"), lax.axis_size("lon")
    owned = count // groups
    half = owned // 2
    assert cols == WC and owned <= 128
    sizes = (qkv_weight.shape[2], proj_weight.shape[1], up_weight.shape[2], down_weight.shape[1])
    n_attn, n_mlp = sizes[0] + sizes[1], sizes[2] + sizes[3]
    inner = inner_factor(lons)
    outer = lons // inner
    pairs = sum(sem_count(outer, inner, parts) for parts in chunk_parts(groups))
    vmem = pl.BlockSpec(memory_space=pltpu.VMEM)
    hbm = pl.BlockSpec(memory_space=pl.ANY)
    tokens = pl.pallas_call(
        functools.partial(kernel, groups, lons, inner, sizes),
        out_shape=jax.ShapeDtypeStruct((groups, owned, width), BF16),
        in_specs=[hbm] * 2 + [vmem] * 3 + [hbm] * 4,
        out_specs=vmem,
        scratch_shapes=[
            pltpu.VMEM((chans, count, width_p), BF16),
            pltpu.VMEM(embed_weight.shape, BF16),
            pltpu.VMEM(up_weight.shape, BF16),
            pltpu.VMEM((chans, count, width), F32),
            pltpu.VMEM((groups, owned, width), BF16),
            pltpu.VMEM((groups, 8, 128), F32),
            pltpu.VMEM((groups - 1, 8, 128), F32),
            pltpu.VMEM((groups - 1, owned, width), BF16),
            pltpu.VMEM((lons, n_attn, width), BF16),
            pltpu.VMEM((lons, n_mlp, width), BF16),
            pltpu.VMEM((lons, n_attn, width), BF16),
            pltpu.VMEM((lons, n_mlp, width), BF16),
            pltpu.VMEM((half, width), BF16),
            pltpu.VMEM((half, width), BF16),
            pltpu.VMEM((2, half, width), BF16),
            pltpu.VMEM((groups, 2, half, width), BF16),
            pltpu.SemaphoreType.DMA((pairs,)),
            pltpu.SemaphoreType.DMA((pairs,)),
            pltpu.SemaphoreType.DMA((8,)),
            pltpu.SemaphoreType.DMA((groups - 1,)),
            pltpu.SemaphoreType.DMA((groups - 1,)),
            pltpu.SemaphoreType.DMA((groups - 1,)),
            pltpu.SemaphoreType.DMA((groups - 1,)),
            pltpu.SemaphoreType.DMA((1,)),
            pltpu.SemaphoreType.DMA((1,)),
            pltpu.SemaphoreType.DMA((groups, 2)),
            pltpu.SemaphoreType.DMA((groups, 2)),
            pltpu.SemaphoreType.DMA((2,)),
        ],
        compiler_params=pltpu.CompilerParams(
            collective_id=0, has_side_effects=True, vmem_limit_bytes=60 * 1024 * 1024
        ),
    )(
        patches.reshape(chans, count, width_p), embed_weight, channel_embed, agg_query.reshape(1, width),
        norm_gains, qkv_weight.transpose(0, 2, 1), proj_weight, up_weight, down_weight,
    )
    decoded = jnp.einsum(
        "te,cep->ctp", tokens.reshape(count, width), decode_weight, preferred_element_type=F32
    ).astype(BF16)
    return decoded.reshape(chans, rows, cols, -1)


def solution(mesh):
    placed = (
        P("chan", None, "lon", None),
        P("chan", None, None),
        P("chan", None),
        P(),
        P(),
        P(None, None, "lon"),
        P(None, "lon", None),
        P(None, None, "lon"),
        P(None, "lon", None),
        P("chan", None, None),
    )
    return jax.shard_map(
        body, mesh=mesh, in_specs=placed, out_specs=P("chan", None, "lon", None), check_vma=False
    )
```
